512 devices in a mesh: rep: 8 (over z), exp: 64 (over y, x, core).
Axes of the slice: x: 4, y: 8, z: 8, core: 2. Of those that a mesh axis runs over, the one named last changes fastest.
Arguments:
- tokens: bfloat16 [81920, 512], P(('rep', 'exp')), may hold values from -6 to 6
- gates: bfloat16 [81920, 2], P(('rep', 'exp')), may hold values from 0.19921875 to 1
- routes: int32 [81920, 2], P(('rep', 'exp')), may hold values from 0 to 63, all different within a row; in each aligned block of 160 rows (0 to 159, 160 to 319, ...) at most 7 rows name the same one
- cotangent: bfloat16 [81920, 512], P(('rep', 'exp')), may hold values from -6 to 6
- w_up: bfloat16 [64, 2048, 512], P('exp'), may hold values from -0.25 to 0.25
- w_down: bfloat16 [64, 2048, 512], P('exp'), may hold values from -0.125 to 0.125
Outputs:
- d_tokens: bfloat16 [81920, 512], P(('rep', 'exp'))
- d_gates: bfloat16 [81920, 2], P(('rep', 'exp'))
- grad_up: bfloat16 [64, 2048, 512], P('exp', 'rep')
- grad_down: bfloat16 [64, 2048, 512], P('exp', 'rep')
The draws below stay inside these ranges and needn't reach their ends.
Inputs may be any that keep to these rules, and one draw needn't show every extreme that they name: `routes`: each row names two different experts. In each aligned block of 160 rows (the rows of one device) no expert is named by more than 7 rows, a bound that some block reaches.
All inputs are finite; a program needn't handle non-finite values.
Results may differ from the reference program's by a relative error of at most 0.014.
Values may be sent and summed in bfloat16 or wider, within the bound.
A program may use at most 64 MiB of HBM per device.

```python
import math
import jax
import jax.numpy as jnp
import numpy as np
from jax import lax

D = 512
FF = 2048
T_DEV = 160
EXPERTS = 64
CAP = 7
TOKENS = 81920
N_REP = 8
N_EXP = 64


def levels(rng, extent, shards, low, top_value):
    level = 1.0
    for position, parts in shards:
        draws = jax.random.uniform(jax.random.fold_in(jax.random.fold_in(rng, 6), position), (parts,), jnp.float32, low / len(shards), top_value / len(shards))
        level = level * jnp.repeat(jnp.exp(draws), extent[position] // parts).reshape((-1,) + (1,) * (len(extent) - 1 - position))
    return level


def shared_out(own_key, own, number, rows, number_of, top, limit, lean):
    order = jax.random.permutation(own_key, number_of)
    heavy_load, common = shares(number_of, rows * top, limit, lean, True), shares(number_of, rows * top, limit, lean, False)
    places = jnp.arange(number_of)

    def named(sizes, turn):
        used = int((sizes > 0).sum())
        fixed = max(1, used // 4)
        passed = fixed + (places - fixed + turn * (used - fixed)) % max(1, number_of - fixed)
        return jnp.zeros((number_of,), jnp.int32).at[order[jnp.where(places < fixed, places, passed)]].set(jnp.asarray(sizes, jnp.int32))

    sizes = jnp.where(number % 4 == 0, named(heavy_load, number // 4), named(common, number - number // 4 - 1))
    mixed = jax.random.permutation(jax.random.fold_in(own, 3), number_of)
    giver, sink = mixed[0:number_of // 2 * 2:2], mixed[1:number_of // 2 * 2:2]
    margin = jnp.minimum(sizes[giver] - 1, limit - sizes[sink]) // 2
    margin = jnp.where((giver == order[0]) | (sink == order[0]) | (sizes[sink] == 0), 0, jnp.maximum(margin, 0))
    passed = jax.random.randint(jax.random.fold_in(own, 4), (number_of // 2,), 0, 1 << 20) % (margin + 1)
    sizes = sizes.at[giver].add(-passed).at[sink].add(passed)
    labels = jnp.searchsorted(jnp.cumsum(sizes), jnp.arange(rows * top), side="right").astype(jnp.int32)
    listing = labels.reshape(top, rows).T
    listing = listing[jax.random.permutation(jax.random.fold_in(own, 1), rows)]
    turn = jax.random.randint(jax.random.fold_in(own, 2), (rows, 1), 0, top)
    return jnp.take_along_axis(listing, (jnp.arange(top)[None, :] + turn) % top, axis=1)


def shares(amount, total, limit, lean, full):
    weights = [(1 << 20) // math.isqrt(standing ** lean) + 1 for standing in range(1, amount + 1)]
    largest = limit if full else min(limit, max(-(-total // amount), total * weights[0] // sum(weights)))
    least = 1 if total - largest >= amount - 1 else 0
    holding, surplus = [largest] + [least] * (amount - 1), total - largest - least * (amount - 1)
    while surplus > 0:
        candidates = [i for i in range(1, amount) if holding[i] < largest] or [i for i in range(1, amount) if holding[i] < limit]
        mass, budget = sum([weights[i] for i in candidates]), surplus
        for i in candidates:
            extra = min(limit - holding[i], max(1, budget * weights[i] // mass), surplus)
            holding[i] = holding[i] + extra
            surplus = surplus - extra
    return np.array(holding)


def scatter_about(own_key, shape, width, reach, shards=(), held_as=jnp.bfloat16):
    loudness = levels(own_key, shape, shards, -0.22, 0.18) if shards else 1.0
    drawn = jax.random.normal(own_key, shape, jnp.float32) * width * loudness
    return jnp.minimum(jnp.maximum(drawn, -reach), reach).astype(held_as)


def setup_inputs(seed: int = 0) -> dict:
    streams_of = jax.random.split(jax.random.key(seed), 7)
    tokens = scatter_about(streams_of[0], (TOKENS, D), 1.0, 6.0, ((0, 512),))
    gates = jnp.clip(0.19921875 + 0.80078125 * jax.random.uniform(streams_of[1], (TOKENS, 2), jnp.float32) ** levels(streams_of[1], (TOKENS, 2), ((0, 512),), -0.2, 0.2), 0.19921875, 1.0).astype(jnp.bfloat16)
    routes_keys = jax.random.split(jax.random.fold_in(streams_of[2], 1), TOKENS // T_DEV)
    routes_turns = jax.random.permutation(jax.random.fold_in(streams_of[2], 3), TOKENS // T_DEV)
    routes = jax.vmap(lambda own, number: shared_out(jax.random.fold_in(streams_of[2], 2), own, number, T_DEV, EXPERTS, 2, CAP, 1))(routes_keys, routes_turns).reshape((TOKENS, 2))
    cotangent = scatter_about(streams_of[3], (TOKENS, D), 1.0, 6.0, ((0, 512),))
    w_up = scatter_about(streams_of[4], (EXPERTS, FF, D), D ** -0.5, 0.25, ((0, 64),))
    w_down = scatter_about(streams_of[5], (EXPERTS, FF, D), FF ** -0.5, 0.125, ((0, 64),))
    return {"tokens": tokens, "gates": gates, "routes": routes, "cotangent": cotangent, "w_up": w_up, "w_down": w_down}


def silu_parts(preact):
    sigma = jax.nn.sigmoid(preact)
    return preact * sigma, sigma * (1.0 + preact * (1.0 - sigma))


def expert_pass(operands):
    up_mat, down_mat, rows_in, grad_in, gate_in = operands
    preact = jnp.dot(rows_in, up_mat.T, preferred_element_type=jnp.float32)
    active, slopes = silu_parts(preact)
    hidden = active.astype(jnp.bfloat16)
    output = jnp.dot(hidden, down_mat, preferred_element_type=jnp.float32)
    gate_grad = jnp.sum(grad_in.astype(jnp.float32) * output, axis=1).astype(jnp.bfloat16)
    out_grad = (gate_in.astype(jnp.float32)[:, None] * grad_in.astype(jnp.float32)).astype(jnp.bfloat16)
    hid_grad = (jnp.dot(out_grad, down_mat.T, preferred_element_type=jnp.float32) * slopes).astype(jnp.bfloat16)
    in_grad = jnp.dot(hid_grad, up_mat, preferred_element_type=jnp.float32).astype(jnp.bfloat16)
    up_part = jnp.dot(hid_grad.T, rows_in, preferred_element_type=jnp.float32).astype(jnp.bfloat16)
    down_part = jnp.dot(hidden.T, out_grad, preferred_element_type=jnp.float32).astype(jnp.bfloat16)
    return in_grad, gate_grad, up_part, down_part


def reference(tokens, gates, routes, cotangent, w_up, w_down):
    per_mirror = N_EXP * T_DEV
    slots_all = N_EXP * CAP

    def mirror_step(totals, operands):
        tok_part, gate_part, route_part, cot_part = operands
        tok_rows = tok_part.shape[0]
        assigned = 2 * tok_rows
        flat_ids = route_part.reshape(-1).astype(jnp.int32)
        onehot = (flat_ids[:, None] == jnp.arange(EXPERTS).astype(jnp.int32)[None, :]).astype(jnp.int32)
        slot_pos = jnp.sum((jnp.cumsum(onehot, axis=0) - 1) * onehot, axis=1).astype(jnp.int32)
        source = jnp.full((EXPERTS, slots_all), assigned, jnp.int32)
        source = source.at[flat_ids, slot_pos].set(jnp.arange(assigned).astype(jnp.int32))
        padded_tok = jnp.concatenate([tok_part, jnp.zeros((1, D), tok_part.dtype)], axis=0)
        padded_cot = jnp.concatenate([cot_part, jnp.zeros((1, D), cot_part.dtype)], axis=0)
        padded_gate = jnp.concatenate([gate_part.reshape(-1), jnp.zeros((1,), gate_part.dtype)], axis=0)
        rows_in = padded_tok[source // 2]
        grad_in = padded_cot[source // 2]
        gate_in = padded_gate[source]
        in_grad, gate_grad, up_part, down_part = lax.map(expert_pass, (w_up, w_down, rows_in, grad_in, gate_in))
        flat_source = source.reshape(-1)
        tok_grad = jnp.zeros((assigned + 1, D), jnp.float32).at[flat_source].add(in_grad.reshape(-1, D).astype(jnp.float32))
        tok_grad = tok_grad[:assigned].reshape(tok_rows, 2, D).sum(axis=1).astype(jnp.bfloat16)
        gate_out = jnp.zeros((assigned + 1,), jnp.bfloat16).at[flat_source].set(gate_grad.reshape(-1))
        gate_out = gate_out[:assigned].reshape(tok_rows, 2)
        totals = (totals[0] + up_part.astype(jnp.float32), totals[1] + down_part.astype(jnp.float32))
        return totals, (tok_grad, gate_out)

    def split(array):
        return array.reshape((N_REP, per_mirror) + array.shape[1:])

    start = (jnp.zeros((EXPERTS, FF, D), jnp.float32), jnp.zeros((EXPERTS, FF, D), jnp.float32))
    totals, outs = lax.scan(mirror_step, start, (split(tokens), split(gates), split(routes), split(cotangent)))
    tok_grads, gate_grads = outs
    return (tok_grads.reshape(TOKENS, D), gate_grads.reshape(TOKENS, 2),
            totals[0].astype(jnp.bfloat16), totals[1].astype(jnp.bfloat16))
```

```python
import functools
import jax
import jax.numpy as jnp
from jax import lax
from jax.experimental import pallas as pl
from jax.experimental.pallas import tpu as pltpu
from jax.sharding import PartitionSpec as P

MESH = pl.DeviceIdType.MESH
F32, BF16, I32 = jnp.float32, jnp.bfloat16, jnp.int32
SLOT = 8
Y, X, C = 8, 4, 2
PARTS = 2


def mm(a, b):
    return lax.dot_general(a, b, (((1,), (0,)), ((), ())), preferred_element_type=F32)


def mm_nt(a, b):
    return lax.dot_general(a, b, (((1,), (1,)), ((), ())), preferred_element_type=F32)


def mm_tn(a, b):
    return lax.dot_general(a, b, (((0,), (0,)), ((), ())), preferred_element_type=F32)


def iota(shape, dim):
    return lax.broadcasted_iota(I32, shape, dim)


def peer_of(me, k):
    a = k % Y
    dy = lax.rem(Y + ((a + 1) // 2) * (2 * (a % 2) - 1), Y)
    b = k // Y
    y = lax.rem(me // (X * C) + dy, Y)
    x = lax.rem((me // C) % X + b // C, X)
    c = lax.rem(me % C + b % C, C)
    return (y * X + x) * C + c


def kernel(
    tok_ref, gate_ref, route_ref, cot_ref, wu_hbm, wd_hbm,
    dtok_ref, dgate_ref, gup_ref, gdn_ref,
    wu, wd, snd, rcv, xs, gs, hid, hgr, acc, dg, bsnd, brcv,
    usnd, dsnd, urcv, drcv,
    wsem, ssem, rsem, bssem, brsem, us, ur, ds, dr,
):
    z = lax.axis_index("rep")
    me = lax.axis_index("exp")
    nz = usnd.shape[0] + 1
    n = snd.shape[0]
    tok_rows, feat = tok_ref.shape
    slots = n * SLOT
    ff = wu.shape[0] // nz
    part = ff // PARTS
    nxt, prv = lax.rem(z + 1, nz), lax.rem(z + nz - 1, nz)

    barrier = pltpu.get_barrier_semaphore()

    @pl.loop(1, n)
    def _(k):
        pl.semaphore_signal(barrier, inc=1, device_id=(z, peer_of(me, k)), device_id_type=MESH)

    pl.semaphore_signal(barrier, inc=1, device_id=(nxt, me), device_id_type=MESH)
    pl.semaphore_signal(barrier, inc=1, device_id=(prv, me), device_id_type=MESH)
    wcopies = [
        pltpu.make_async_copy(wu_hbm.at[0], wu, wsem.at[0]),
        pltpu.make_async_copy(wd_hbm.at[0], wd, wsem.at[1]),
    ]
    for copy in wcopies:
        copy.start()

    routes = route_ref[...]
    gates = gate_ref[...].astype(F32)
    cot = cot_ref[...].astype(F32)
    expert = iota((tok_rows, n), 1)
    hot = [routes[:, k : k + 1] == expert for k in range(2)]
    both = jnp.logical_or(hot[0], hot[1]).astype(F32).astype(BF16)
    row_i, col_i = iota((tok_rows, tok_rows), 0), iota((tok_rows, tok_rows), 1)
    before = mm((row_i > col_i).astype(F32).astype(BF16), both)
    pos = [jnp.sum(jnp.where(h, before, 0.0), axis=1, keepdims=True) for h in hot]
    target = [routes[:, k : k + 1].astype(F32) * SLOT + pos[k] for k in range(2)]
    slot_i = iota((slots, tok_rows), 0).astype(F32)
    sel = []
    for k in range(2):
        as_row = jnp.sum(jnp.where(row_i == col_i, target[k], 0.0), axis=0, keepdims=True)
        sel.append((slot_i == as_row).astype(F32))
    rows = mm((sel[0] + sel[1]).astype(BF16), tok_ref[...])
    grads = mm(sel[0].astype(BF16), (gates[:, 0:1] * cot).astype(BF16))
    grads += mm(sel[1].astype(BF16), (gates[:, 1:2] * cot).astype(BF16))
    snd[:, 0] = rows.reshape(n, SLOT, feat).astype(BF16)
    snd[:, 1] = grads.reshape(n, SLOT, feat).astype(BF16)
    rcv[me] = snd[me]

    pl.semaphore_wait(barrier, n + 1)

    @pl.loop(1, n)
    def _(k):
        peer = peer_of(me, k)
        pltpu.make_async_remote_copy(
            src_ref=snd.at[peer], dst_ref=rcv.at[me], send_sem=ssem, recv_sem=rsem,
            device_id=(z, peer), device_id_type=MESH,
        ).start()

    acc[...] = jnp.zeros_like(acc)
    dg[...] = jnp.zeros_like(dg)
    for copy in wcopies:
        copy.wait()
    others = pl.ds(0, n - 1)
    pltpu.make_async_copy(rcv.at[others], rcv.at[others], rsem).wait()
    xs[...] = rcv[:, 0].astype(F32).reshape(slots, feat).astype(BF16)
    gs[...] = rcv[:, 1].astype(F32).reshape(slots, feat).astype(BF16)

    def expert_part(order):
        half = order // 2 + 1
        off = (2 * (order % 2) - 1) * half + (order // (nz - 1)) * (nz // 2)
        at = pl.ds(pl.multiple_of(lax.rem(z + nz + off, nz) * ff, ff), ff)
        up, down = wu[at, :], wd[at, :]
        pre = mm_nt(up, xs[...])
        back = mm_nt(down, gs[...])
        sigma = jax.nn.sigmoid(pre)
        hidden = (pre * sigma).astype(BF16)
        slope = sigma * (1.0 + pre * (1.0 - sigma))
        grad = (back * slope).astype(BF16)
        hid[at, :] = hidden
        hgr[at, :] = grad
        dg[...] += jnp.sum((hidden.astype(F32) * back).reshape(ff // 8, 8, slots), axis=0)
        acc[...] += mm_tn(grad, up)

    def ring(step, c, up):
        snd_buf, rcv_buf, s_sem, r_sem = (usnd, urcv, us, ur) if up else (dsnd, drcv, ds, dr)
        at = pl.ds(c * part, part)
        return pltpu.make_async_remote_copy(
            src_ref=snd_buf.at[step, at], dst_ref=rcv_buf.at[step, at],
            send_sem=s_sem.at[step, c], recv_sem=r_sem.at[step, c],
            device_id=(nxt if up else prv, me), device_id_type=MESH,
        )

    def partial(shard, c, up):
        at = pl.ds(pl.multiple_of(shard * ff + c * part, part), part)
        return mm(hgr[at, :], xs[...]) if up else mm(hid[at, :], gs[...])

    def ring_step(step, first):
        for c in range(PARTS):
            for up in (True, False):
                shard = lax.rem(z + nz - 1 - step, nz) if up else lax.rem(z + 1 + step, nz)
                value = partial(shard, c, up)
                at = pl.ds(c * part, part)
                if not first:
                    ring(step - 1, c, up).wait_recv()
                    value += (urcv if up else drcv)[step - 1, at].astype(F32)
                (usnd if up else dsnd)[step, at] = value.astype(BF16)
                ring(step, c, up).start()

    def two_parts(step):
        @pl.loop(0, 2)
        def _(k):
            expert_part(2 * step + k)

    two_parts(0)
    ring_step(0, True)

    @pl.loop(1, nz // 2)
    def _(step):
        two_parts(step)
        ring_step(step, False)

    gate_row = jnp.sum(dg[...], axis=0, keepdims=True)
    gi, si = iota((n, slots), 0), iota((n, slots), 1)
    spread = jnp.where(si // SLOT == gi, gate_row, 0.0).astype(BF16)
    lane = iota((slots, feat), 1)
    place = (iota((slots, feat), 0) % SLOT == lane).astype(F32).astype(BF16)
    gate_out = mm(spread, place)
    packed = acc[...].reshape(n, SLOT, feat)
    packed = jnp.where(iota((n, SLOT, feat), 1) == SLOT - 1, gate_out[:, None, :], packed)
    bsnd[...] = packed.astype(BF16)
    brcv[me] = bsnd[me]

    @pl.loop(1, n)
    def _(k):
        peer = peer_of(me, k)
        pltpu.make_async_remote_copy(
            src_ref=bsnd.at[peer], dst_ref=brcv.at[me], send_sem=bssem, recv_sem=brsem,
            device_id=(z, peer), device_id_type=MESH,
        ).start()

    @pl.loop(nz // 2, nz - 1)
    def _(step):
        ring_step(step, False)

    pltpu.make_async_copy(brcv.at[others], brcv.at[others], brsem).wait()
    slot_l = iota((tok_rows, slots), 1).astype(F32)
    owned = jnp.logical_or(slot_l == target[0], slot_l == target[1]).astype(F32).astype(BF16)
    returned = brcv[...].astype(F32).reshape(slots, feat).astype(BF16)
    dtok_ref[...] = mm(owned, returned).astype(BF16)
    gate_back = brcv[:, SLOT - 1, 0:128]
    lane_i = iota((tok_rows, 128), 1).astype(F32)
    gates_out = []
    for k in range(2):
        rows_k = mm(hot[k].astype(F32).astype(BF16), gate_back)
        value = jnp.sum(jnp.where(lane_i == pos[k], rows_k, 0.0), axis=1, keepdims=True)
        gates_out.append(value / gates[:, k : k + 1])
    col = iota((tok_rows, 2), 1)
    dgate_ref[...] = jnp.where(col == 0, gates_out[0], gates_out[1]).astype(BF16)

    last = nz - 2
    for c in range(PARTS):
        at = pl.ds(c * part, part)
        for up in (True, False):
            value = partial(z, c, up)
            ring(last, c, up).wait_recv()
            value += (urcv if up else drcv)[last, at].astype(F32)
            (gup_ref if up else gdn_ref)[0, at] = value.astype(BF16)

    pltpu.make_async_copy(snd.at[others], snd.at[others], ssem).wait()
    pltpu.make_async_copy(bsnd.at[others], bsnd.at[others], bssem).wait()

    @pl.loop(0, nz - 1)
    def _(step):
        for c in range(PARTS):
            for up in (True, False):
                ring(step, c, up).wait_send()


def local(tokens, gates, routes, cotangent, w_up, w_down):
    tok_rows, feat = tokens.shape
    n = lax.axis_size("exp")
    nz = lax.axis_size("rep")
    hidden = w_up.shape[1]
    ff = hidden // nz
    slots = n * SLOT
    vmem = pl.BlockSpec(memory_space=pltpu.VMEM)
    hbm = pl.BlockSpec(memory_space=pl.ANY)
    V = pltpu.VMEM
    dma = pltpu.SemaphoreType.DMA
    return pl.pallas_call(
        kernel,
        out_shape=(
            jax.ShapeDtypeStruct((tok_rows, feat), BF16),
            jax.ShapeDtypeStruct((tok_rows, 2), BF16),
            jax.ShapeDtypeStruct((1, ff, feat), BF16),
            jax.ShapeDtypeStruct((1, ff, feat), BF16),
        ),
        in_specs=[vmem, vmem, vmem, vmem, hbm, hbm],
        out_specs=(vmem, vmem, vmem, vmem),
        scratch_shapes=[
            V((hidden, feat), BF16), V((hidden, feat), BF16),
            V((n, 2, SLOT, feat), BF16), V((n, 2, SLOT, feat), BF16),
            V((slots, feat), BF16), V((slots, feat), BF16),
            V((hidden, slots), BF16), V((hidden, slots), BF16),
            V((slots, feat), F32), V((8, slots), F32),
            V((n, SLOT, feat), BF16), V((n, SLOT, feat), BF16),
        ]
        + [V((nz - 1, ff, feat), BF16)] * 4
        + [dma((2,)), dma, dma, dma, dma]
        + [dma((nz - 1, PARTS))] * 4,
        compiler_params=pltpu.CompilerParams(
            collective_id=0, has_side_effects=True, vmem_limit_bytes=60 * 2**20
        ),
        name="expert_backward",
    )(tokens, gates, routes, cotangent, w_up, w_down)


def solution(mesh):
    in_specs = (
        P(("rep", "exp"), None),
        P(("rep", "exp"), None),
        P(("rep", "exp"), None),
        P(("rep", "exp"), None),
        P("exp", None, None),
        P("exp", None, None),
    )
    out_specs = (
        P(("rep", "exp"), None),
        P(("rep", "exp"), None),
        P("exp", "rep", None),
        P("exp", "rep", None),
    )
    return jax.shard_map(local, mesh=mesh, in_specs=in_specs, out_specs=out_specs, check_vma=False)
```

```python
import functools
import jax
import jax.numpy as jnp
from jax import lax
from jax.experimental import pallas as pl
from jax.experimental.pallas import tpu as pltpu
from jax.sharding import PartitionSpec as P

MESH = pl.DeviceIdType.MESH
F32, BF16, I32 = jnp.float32, jnp.bfloat16, jnp.int32
CAP, SLOT, LANE = 7, 8, 128
Y, X, C = 8, 4, 2
ROW = X * C
PARTS = 2
LONG, SHORT = 3, 2


def mm(a, b):
    return lax.dot_general(a, b, (((1,), (0,)), ((), ())), preferred_element_type=F32)


def mm_nt(a, b):
    return lax.dot_general(a, b, (((1,), (1,)), ((), ())), preferred_element_type=F32)


def mm_tn(a, b):
    return lax.dot_general(a, b, (((0,), (0,)), ((), ())), preferred_element_type=F32)


def iota(shape, dim):
    return lax.broadcasted_iota(I32, shape, dim)


def mask16(m):
    return m.astype(F32).astype(BF16)


def kernel(
    tok_ref, gate_ref, route_ref, cot_ref, wu_hbm, wd_hbm,
    dtok_ref, dgate_ref, gup_ref, gdn_ref,
    wu, wd, snd, rcv, nb, pack, tmp, x3, g3, x2, g2, th, tg, acc, dg, ret, bsnd, brcv,
    ring_s, ring_r, base,
    wsem, lsem, ssem, rsem, fs, fr, bssem, brsem, rs, rr,
):
    z = lax.axis_index("rep")
    me = lax.axis_index("exp")
    nz = lax.axis_size("rep")
    n = snd.shape[0]
    tok_rows, feat = tok_ref.shape
    chunks = feat // LANE
    slots = n * SLOT
    ff = wu.shape[0] // nz
    part = ff // PARTS
    nxt, prv = lax.rem(z + 1, nz), lax.rem(z + nz - 1, nz)
    my_y, my_x, my_c = me // ROW, lax.rem(me // C, X), lax.rem(me, C)
    offs = [lax.rem(my_x + b // C, X) * C + lax.rem(my_c + b % C, C) for b in range(ROW)]

    def row_at(a):
        half = (a + 1) // 2
        return lax.rem(my_y + Y + (2 * lax.rem(a, 2) - 1) * half, Y)

    def each_peer(visit):
        for b in range(1, ROW):
            visit(my_y * ROW + offs[b])

        @pl.loop(1, Y)
        def _(a):
            first = row_at(a) * ROW
            for b in range(ROW):
                visit(first + offs[b])

    barrier = pltpu.get_barrier_semaphore()
    each_peer(
        lambda peer: pl.semaphore_signal(
            barrier, inc=1, device_id=(z, peer), device_id_type=MESH
        )
    )
    pl.semaphore_signal(barrier, inc=1, device_id=(nxt, me), device_id_type=MESH)
    pl.semaphore_signal(barrier, inc=1, device_id=(prv, me), device_id_type=MESH)
    wcopies = [
        pltpu.make_async_copy(wu_hbm.at[0], wu, wsem.at[0]),
        pltpu.make_async_copy(wd_hbm.at[0], wd, wsem.at[1]),
    ]
    for copy in wcopies:
        copy.start()

    routes = route_ref[...]
    gates = gate_ref[...].astype(F32)
    row_i, col_i = iota((tok_rows, tok_rows), 0), iota((tok_rows, tok_rows), 1)
    eye = row_i == col_i

    def column(v):
        return jnp.sum(jnp.where(eye, v, 0.0), axis=1, keepdims=True)

    expert = iota((n, tok_rows), 0)
    ids = [routes[k : k + 1, :] for k in range(2)]
    hot = [ids[k] == expert for k in range(2)]
    before = mm(mask16(jnp.logical_or(hot[0], hot[1])), mask16(row_i < col_i))
    pos = [jnp.sum(jnp.where(h, before, 0.0), axis=0, keepdims=True) for h in hot]
    slot_i = iota((n * CAP, tok_rows), 0).astype(F32)
    sel = [(slot_i == pos[k] * n + ids[k].astype(F32)).astype(F32) for k in range(2)]
    cot = cot_ref[...].astype(F32)
    rows = mm((sel[0] + sel[1]).astype(BF16), tok_ref[...])
    grads = mm(sel[0].astype(BF16), (column(gates[0:1, :]) * cot).astype(BF16))
    grads += mm(sel[1].astype(BF16), (column(gates[1:2, :]) * cot).astype(BF16))
    for s in range(CAP):
        for r in range(chunks):
            at = slice(r * LANE, (r + 1) * LANE)
            pack[s, pl.ds(r, n, stride=SLOT), :] = rows[s * n : (s + 1) * n, at]
            pack[s, pl.ds(chunks + r, n, stride=SLOT), :] = grads[s * n : (s + 1) * n, at]
    for s in range(CAP):
        snd[:, :, s * LANE : (s + 1) * LANE] = pack[s].reshape(n, SLOT, LANE).astype(BF16)

    pl.semaphore_wait(barrier, n + 1)
    own = pltpu.make_async_copy(snd.at[me], rcv.at[me], lsem)
    own.start()
    each_peer(
        lambda peer: pltpu.make_async_remote_copy(
            src_ref=snd.at[peer], dst_ref=rcv.at[me], send_sem=ssem, recv_sem=rsem.at[my_y],
            device_id=(z, peer), device_id_type=MESH,
        ).start()
    )

    x3[:, ROW * CAP :] = jnp.zeros_like(x3[:, ROW * CAP :])
    g3[:, ROW * CAP :] = jnp.zeros_like(g3[:, ROW * CAP :])
    acc[...] = jnp.zeros_like(acc)
    dg[...] = jnp.zeros_like(dg)

    def forward(side, g):
        at = pl.ds(g * ROW, ROW)
        return pltpu.make_async_remote_copy(
            src_ref=rcv.at[at], dst_ref=nb.at[side, at], send_sem=fs, recv_sem=fr.at[side, g],
            device_id=((nxt, prv)[side], me), device_id_type=MESH,
        )

    def unpack(block, m, g):
        for s in range(CAP):
            tile = block[:, :, s * LANE : (s + 1) * LANE].astype(F32)
            tmp[s] = tile.reshape(ROW * SLOT, LANE)
        for s in range(CAP):
            for r in range(chunks):
                at = slice(r * LANE, (r + 1) * LANE)
                x3[m, s * Y + g, :, at] = tmp[s, pl.ds(r, ROW, stride=SLOT), :].astype(BF16)
                g3[m, s * Y + g, :, at] = tmp[s, pl.ds(chunks + r, ROW, stride=SLOT), :].astype(BF16)

    def arrived(a, count):
        g = row_at(a)
        got = rcv.at[pl.ds(0, count)]
        pltpu.make_async_copy(got, got, rsem.at[g]).wait()
        forward(0, g).start()
        forward(1, g).start()
        unpack(rcv[pl.ds(g * ROW, ROW)], 1, g)

    def flat(m):
        x2[m] = x3[m].astype(F32).reshape(slots, feat).astype(BF16)
        g2[m] = g3[m].astype(F32).reshape(slots, feat).astype(BF16)

    def neighbours(a):
        g = row_at(a)
        for side in range(2):
            forward(side, g).wait_recv()
            unpack(nb[side, pl.ds(g * ROW, ROW)], 2 * side, g)

    own.wait()
    arrived(0, ROW - 1)

    @pl.loop(1, Y)
    def _(a):
        arrived(a, ROW)

    for copy in wcopies:
        copy.wait()
    flat(1)

    def front(m, shard):
        at = pl.ds(pl.multiple_of(shard * ff, ff), ff)
        up = wu[at, :]
        pre = mm_nt(up, x2[m])
        back = mm_nt(wd[at, :], g2[m])
        sigma = jax.nn.sigmoid(pre)
        hidden = (pre * sigma).astype(BF16)
        grad = (back * (sigma * (1.0 + pre * (1.0 - sigma)))).astype(BF16)
        return up, hidden, grad, back

    def own_part(shard, save):
        up, hidden, grad, back = front(1, shard)
        if save:
            th[2 * LONG + 2] = hidden
            tg[2 * LONG + 2] = grad
        dg[...] += jnp.sum((hidden.astype(F32) * back).reshape(ff // 8, 8, slots), axis=0)
        acc[...] += mm_tn(grad, up)

    def side_parts(j):
        for side in (1, 0):
            shard = lax.rem(z + nz - LONG + j, nz) if side else lax.rem(z + LONG - j, nz)
            _, hidden, grad, _ = front(2 * side, shard)
            th[(LONG + 1) * side + j] = hidden
            tg[(LONG + 1) * side + j] = grad

    own_part(z, True)

    @pl.loop(0, Y - 2)
    def _(a):
        neighbours(a)

    own_part(lax.rem(z + 1, nz), False)

    @pl.loop(Y - 2, Y)
    def _(a):
        neighbours(a)

    flat(2)
    flat(0)

    def product(is_up, m, idx, at):
        return mm(tg[idx, at], x2[m]) if is_up else mm(th[idx, at], g2[m])

    def hop(side, slot, c):
        at = pl.ds(c * part, part)
        return pltpu.make_async_remote_copy(
            src_ref=ring_s.at[side, slot, at], dst_ref=ring_r.at[side, slot, at],
            send_sem=rs.at[side, slot, c], recv_sem=rr.at[side, slot, c],
            device_id=((nxt, prv)[side], me), device_id_type=MESH,
        )

    def send(is_long, j):
        slot = j if is_long else SHORT + j
        first = j == 0 if is_long else j == 1
        for c in range(PARTS):
            at = pl.ds(c * part, part)
            for side in (1, 0):
                value = product(is_long == (side == 1), 2 * side, (LONG + 1) * side + j, at)
                if not first:
                    hop(side, slot - 1, c).wait_recv()
                    value += ring_r[side, slot - 1, at].astype(F32)
                ring_s[side, slot, at] = value.astype(BF16)
                hop(side, slot, c).start()

    side_parts(0)
    send(True, 0)
    side_parts(1)
    send(False, 1)

    @pl.loop(2, nz)
    def _(i):
        own_part(lax.rem(z + i, nz), False)

    gate_row = jnp.sum(dg[...], axis=0, keepdims=True)
    spread = jnp.where(iota((n, slots), 1) % n == iota((n, slots), 0), gate_row, 0.0)
    place = mask16(iota((slots, LANE), 0) // n == iota((slots, LANE), 1))
    gate_out = mm(spread.astype(BF16), place)
    for r in range(chunks):
        at = slice(r * LANE, (r + 1) * LANE)
        for s in range(CAP):
            ret[r, pl.ds(s, n, stride=SLOT), :] = acc[s * n : (s + 1) * n, at]
        ret[r, pl.ds(CAP, n, stride=SLOT), :] = gate_out
    for r in range(chunks):
        bsnd[:, :, r * LANE : (r + 1) * LANE] = ret[r].reshape(n, SLOT, LANE).astype(BF16)
    own_back = pltpu.make_async_copy(bsnd.at[me], brcv.at[me], lsem)
    own_back.start()
    each_peer(
        lambda peer: pltpu.make_async_remote_copy(
            src_ref=bsnd.at[peer], dst_ref=brcv.at[me], send_sem=bssem, recv_sem=brsem,
            device_id=(z, peer), device_id_type=MESH,
        ).start()
    )

    send(True, 1)
    side_parts(2)
    send(False, 2)
    send(True, 2)
    side_parts(3)
    everything = pl.ds(0, ff)
    mine = ((0, LONG), (1, 2 * LONG + 2), (2, 2 * LONG + 1))
    for which in range(2):
        base[which] = sum(product(which == 0, m, idx, everything) for m, idx in mine)

    own_back.wait()
    others = pl.ds(0, n - 1)
    pltpu.make_async_copy(brcv.at[others], brcv.at[others], brsem).wait()
    slot_l = iota((tok_rows, slots), 1).astype(F32)
    places = [column(ids[k].astype(F32) * SLOT + pos[k]) for k in range(2)]
    owned = mask16(jnp.logical_or(slot_l == places[0], slot_l == places[1]))
    returned = brcv[...].astype(F32).reshape(slots, feat).astype(BF16)
    dtok_ref[...] = mm(owned, returned).astype(BF16)
    gate_back = brcv[:, CAP, 0:LANE]
    which_slot = iota((LANE, tok_rows), 0).astype(F32)
    gates_out = []
    for k in range(2):
        mixed = mm_tn(gate_back, mask16(hot[k]))
        value = jnp.sum(jnp.where(which_slot == pos[k], mixed, 0.0), axis=0, keepdims=True)
        gates_out.append(value / gates[k : k + 1, :])
    first_row = iota((2, tok_rows), 0) == 0
    dgate_ref[...] = jnp.where(first_row, gates_out[0], gates_out[1]).astype(BF16)

    for c in range(PARTS):
        at = pl.ds(c * part, part)
        for side in (1, 0):
            hop(side, LONG + SHORT - 1, c).wait_recv()
            base[side, at] += ring_r[side, LONG + SHORT - 1, at].astype(F32)
        for side in (1, 0):
            hop(side, LONG - 1, c).wait_recv()
            value = base[1 - side, at] + ring_r[side, LONG - 1, at].astype(F32)
            (gup_ref if side else gdn_ref)[0, at] = value.astype(BF16)

    pltpu.make_async_copy(snd.at[others], snd.at[others], ssem).wait()
    pltpu.make_async_copy(bsnd.at[others], bsnd.at[others], bssem).wait()
    pltpu.make_async_copy(nb, nb, fs).wait()
    for side in range(2):
        for slot in range(LONG + SHORT):
            for c in range(PARTS):
                hop(side, slot, c).wait_send()


def finish(*refs):
    for src, dst in zip(refs[:4], refs[4:]):
        dst[...] = src[...]


def local(tokens, gates, routes, cotangent, w_up, w_down):
    tok_rows, feat = tokens.shape
    n = lax.axis_size("exp")
    nz = lax.axis_size("rep")
    hidden = w_up.shape[1]
    ff = hidden // nz
    slots = n * SLOT
    vmem = pl.BlockSpec(memory_space=pltpu.VMEM)
    hbm = pl.BlockSpec(memory_space=pl.ANY)
    V = pltpu.VMEM
    dma = pltpu.SemaphoreType.DMA
    hops = LONG + SHORT
    tiles = 2 * LONG + 3
    shapes = (
        jax.ShapeDtypeStruct((tok_rows, feat), BF16),
        jax.ShapeDtypeStruct((2, tok_rows), BF16),
        jax.ShapeDtypeStruct((1, ff, feat), BF16),
        jax.ShapeDtypeStruct((1, ff, feat), BF16),
    )
    outs = pl.pallas_call(
        kernel,
        out_shape=shapes,
        in_specs=[vmem, vmem, vmem, vmem, hbm, hbm],
        out_specs=(vmem, vmem, vmem, vmem),
        scratch_shapes=[
            V((hidden, feat), BF16), V((hidden, feat), BF16),
            V((n, SLOT, CAP * LANE), BF16), V((n, SLOT, CAP * LANE), BF16),
            V((2, n, SLOT, CAP * LANE), BF16),
            V((CAP, n * SLOT, LANE), F32), V((CAP, ROW * SLOT, LANE), F32),
            V((3, n, SLOT, feat), BF16), V((3, n, SLOT, feat), BF16),
            V((3, slots, feat), BF16), V((3, slots, feat), BF16),
            V((tiles, ff, slots), BF16), V((tiles, ff, slots), BF16),
            V((slots, feat), F32), V((8, slots), F32),
            V((feat // LANE, slots, LANE), F32),
            V((n, SLOT, feat), BF16), V((n, SLOT, feat), BF16),
            V((2, hops, ff, feat), BF16), V((2, hops, ff, feat), BF16),
            V((2, ff, feat), F32),
            dma((2,)), dma, dma, dma((Y,)), dma, dma((2, Y)), dma, dma,
            dma((2, hops, PARTS)), dma((2, hops, PARTS)),
        ],
        compiler_params=pltpu.CompilerParams(
            collective_id=0, has_side_effects=True, vmem_limit_bytes=60 * 2**20
        ),
        name="expert_backward",
    )(tokens, gates.T, routes.T, cotangent, w_up, w_down)
    d_tokens, d_gates, grad_up, grad_down = pl.pallas_call(
        finish,
        out_shape=shapes,
        in_specs=[vmem] * 4,
        out_specs=(vmem,) * 4,
        compiler_params=pltpu.CompilerParams(vmem_limit_bytes=4 * 2**20),
        name="finish",
    )(*outs)
    return d_tokens, d_gates.T, grad_up, grad_down


def solution(mesh):
    in_specs = (
        P(("rep", "exp"), None),
        P(("rep", "exp"), None),
        P(("rep", "exp"), None),
        P(("rep", "exp"), None),
        P("exp", None, None),
        P("exp", None, None),
    )
    out_specs = (
        P(("rep", "exp"), None),
        P(("rep", "exp"), None),
        P("exp", "rep", None),
        P("exp", "rep", None),
    )
    return jax.shard_map(local, mesh=mesh, in_specs=in_specs, out_specs=out_specs, check_vma=False)
```
